32 devices in a mesh: cp: 8 (over z, x), tp: 4 (over y, core).
Axes of the slice: x: 2, y: 2, z: 4, core: 2. Of those that a mesh axis runs over, the one named last changes fastest.
Arguments:
- tokens: bfloat16 [4096, 4096], P(('cp', 'tp')), may hold values from -6 to 6
- grad_out: bfloat16 [4096, 4096], P(('cp', 'tp')), may hold values from -6 to 6
- expert_ids: int32 [4096, 1], P(('cp', 'tp')), may hold values from 0 to 7; in each aligned block of 128 rows (0 to 127, 128 to 255, ...) at most 24 rows name the same one
- router_weights: float32 [4096, 1], P(('cp', 'tp')), may hold values from 0.2 to 1
- gate_weight: bfloat16 [8, 1536, 4096], P('cp', 'tp'), may hold values from -0.09375 to 0.09375
- up_weight: bfloat16 [8, 1536, 4096], P('cp', 'tp'), may hold values from -0.09375 to 0.09375
- down_weight: bfloat16 [8, 1536, 4096], P('cp', 'tp'), may hold values from -0.15625 to 0.15625
Outputs:
- grad_tokens: bfloat16 [4096, 4096], P(('cp', 'tp'))
- grad_gate: float32 [8, 1536, 4096], P('cp', 'tp')
- grad_up: float32 [8, 1536, 4096], P('cp', 'tp')
- grad_down: float32 [8, 1536, 4096], P('cp', 'tp')
The draws below stay inside these ranges and needn't reach their ends.
Inputs may be any that keep to these rules, and one draw needn't show every extreme that they name: `expert_ids`: within each aligned block of 128 consecutive rows (rows 0 to 127, 128 to 255, and so on) each expert is named at most 24 times, and in some block some expert is named exactly 24 times.
All inputs are finite; a program needn't handle non-finite values.
Results may differ from the reference program's by a relative error of at most 0.009.
Values may be sent and summed in bfloat16 or wider, within the bound.
A program may use at most 256 MiB of HBM per device.

```python
import math
import jax
import jax.numpy as jnp
import numpy as np
from jax import lax

D = 4096
FF = 1536
TOK_DEV = 128
TOP = 1
EXPERTS = 8
CAP = 24
TOKENS = 4096
N_CP = 8
N_TP = 4


def steps_of(key, extent, split, smallest, top_value):
    def one(position, blocks):
        steps = jax.random.uniform(jax.random.fold_in(jax.random.fold_in(key, 6), position), (blocks,), jnp.float32, smallest / len(split), top_value / len(split))
        return jnp.repeat(jnp.exp(steps), extent[position] // blocks).reshape((-1,) + (1,) * (len(extent) - position - 1))

    level = one(*split[0])
    for cut in split[1:]:
        level = level * one(*cut)
    return level


def shared_out(key, own, number, rows, amount, top, reach, skew):
    sequence = jax.random.permutation(key, amount)
    heavy_load, ordinary = portions_of(amount, rows * top, reach, skew, True), portions_of(amount, rows * top, reach, skew, False)
    places = jnp.arange(amount)

    def named(lengths, turn):
        used = int((lengths > 0).sum())
        fixed = max(1, used // 4)
        passed = fixed + (places - fixed + turn * (used - fixed)) % max(1, amount - fixed)
        return jnp.zeros((amount,), jnp.int32).at[sequence[jnp.where(places < fixed, places, passed)]].set(jnp.asarray(lengths, jnp.int32))

    lengths = jnp.where(number % 4 == 0, named(heavy_load, number // 4), named(ordinary, number - number // 4 - 1))
    mixed = jax.random.permutation(jax.random.fold_in(own, 3), amount)
    giver, sink = mixed[0:amount // 2 * 2:2], mixed[1:amount // 2 * 2:2]
    margin = jnp.minimum(lengths[giver] - 1, reach - lengths[sink]) // 2
    margin = jnp.where((giver == sequence[0]) | (sink == sequence[0]) | (lengths[sink] == 0), 0, jnp.maximum(margin, 0))
    passed = jax.random.randint(jax.random.fold_in(own, 4), (amount // 2,), 0, 1 << 20) % (margin + 1)
    lengths = lengths.at[giver].add(-passed).at[sink].add(passed)
    items = jnp.searchsorted(jnp.cumsum(lengths), jnp.arange(rows * top), side="right").astype(jnp.int32)
    table = items.reshape(top, rows).T
    table = table[jax.random.permutation(jax.random.fold_in(own, 1), rows)]
    turn = jax.random.randint(jax.random.fold_in(own, 2), (rows, 1), 0, top)
    return jnp.take_along_axis(table, (jnp.arange(top)[None, :] + turn) % top, axis=1)


def portions_of(amount, total, bound, skew, full):
    loads = [(1 << 20) // math.isqrt(rank ** skew) + 1 for rank in range(1, amount + 1)]
    largest = bound if full else min(bound, max(-(-total // amount), total * loads[0] // sum(loads)))
    least = 1 if total - largest >= amount - 1 else 0
    holding, spare = [largest] + [least] * (amount - 1), total - largest - least * (amount - 1)
    while spare > 0:
        candidates = [i for i in range(1, amount) if holding[i] < largest] or [i for i in range(1, amount) if holding[i] < bound]
        pool, left = sum([loads[i] for i in candidates]), spare
        for i in candidates:
            more = min(bound - holding[i], max(1, left * loads[i] // pool), spare)
            holding[i] = holding[i] + more
            spare = spare - more
    return np.array(holding)


def noise(rng, extent, width, bound, split=(), kind=jnp.bfloat16):
    factor_of = steps_of(rng, extent, split, -0.22, 0.18) if split else 1.0
    entries = jax.random.normal(rng, extent, jnp.float32) * width * factor_of
    return jnp.minimum(jnp.maximum(entries, -bound), bound).astype(kind)


def setup_inputs(seed: int = 0) -> dict:
    arg_keys = jax.random.split(jax.random.key(seed), 8)
    tokens = noise(arg_keys[0], (TOKENS, D), 1.0, 6.0, ((0, 32),))
    grad_out = noise(arg_keys[1], (TOKENS, D), 1.0, 6.0, ((0, 32),))
    expert_ids_keys = jax.random.split(jax.random.fold_in(arg_keys[2], 1), TOKENS // TOK_DEV)
    expert_ids_turns = jax.random.permutation(jax.random.fold_in(arg_keys[2], 3), TOKENS // TOK_DEV)
    expert_ids = jax.vmap(lambda own, number: shared_out(jax.random.fold_in(arg_keys[2], 2), own, number, TOK_DEV, EXPERTS, TOP, CAP, 1))(expert_ids_keys, expert_ids_turns).reshape((TOKENS, TOP))
    router_weights = jnp.clip(0.2 + 0.8 * jax.random.uniform(arg_keys[3], (TOKENS, TOP), jnp.float32) ** steps_of(arg_keys[3], (TOKENS, TOP), ((0, 32),), -0.2, 0.2), 0.2, 1.0)
    gate_weight = noise(arg_keys[4], (EXPERTS, FF, D), D ** -0.5, 0.09375, ((0, 8), (1, 4)))
    up_weight = noise(arg_keys[5], (EXPERTS, FF, D), D ** -0.5, 0.09375, ((0, 8), (1, 4)))
    down_weight = noise(arg_keys[6], (EXPERTS, FF, D), FF ** -0.5, 0.15625, ((0, 8), (1, 4)))
    return dict(tokens=tokens, grad_out=grad_out, expert_ids=expert_ids, router_weights=router_weights, gate_weight=gate_weight, up_weight=up_weight, down_weight=down_weight)


def reference(tokens, grad_out, expert_ids, router_weights, gate_weight, up_weight, down_weight):
    ndev = N_CP * N_TP
    per_dev = TOK_DEV * TOP
    ids = expert_ids.reshape(ndev, per_dev).astype(jnp.int32)
    onehot = (ids[:, :, None] == jnp.arange(EXPERTS, dtype=jnp.int32)[None, None, :]).astype(jnp.int32)
    before = jnp.cumsum(onehot, axis=1) - onehot
    rank = jnp.sum(before * onehot, axis=2)
    place = jnp.arange(ndev, dtype=jnp.int32)[:, None] * CAP + rank
    flat_ids = ids.reshape(-1)
    flat_place = place.reshape(-1).astype(jnp.int32)
    owner = jnp.full((EXPERTS, ndev * CAP), -1, jnp.int32)
    owner = owner.at[flat_ids, flat_place].set(jnp.arange(TOKENS * TOP, dtype=jnp.int32))
    x_assign = jnp.repeat(tokens, TOP, axis=0)
    g_assign = (router_weights.reshape(-1, 1) * jnp.repeat(grad_out, TOP, axis=0).astype(jnp.float32)).astype(jnp.bfloat16)
    block = FF // N_TP

    def expert(args):
        index_row, w_gate, w_up, w_down = args
        valid = (index_row >= 0)[:, None]
        safe = jnp.maximum(index_row, 0)
        slot_in = jnp.where(valid, x_assign[safe].astype(jnp.float32), jnp.float32(0.0))
        slot_go = jnp.where(valid, g_assign[safe].astype(jnp.float32), jnp.float32(0.0))
        wg32 = w_gate.astype(jnp.float32)
        wu32 = w_up.astype(jnp.float32)
        wd32 = w_down.astype(jnp.float32)
        gate = jnp.dot(slot_in, wg32.T, preferred_element_type=jnp.float32)
        upval = jnp.dot(slot_in, wu32.T, preferred_element_type=jnp.float32)
        sig = jax.nn.sigmoid(gate)
        act = gate * sig
        hidden = lax.optimization_barrier((act * upval).astype(jnp.bfloat16)).astype(jnp.float32)
        grad_hidden = jnp.dot(slot_go, wd32.T, preferred_element_type=jnp.float32)
        grad_upin = lax.optimization_barrier((grad_hidden * act).astype(jnp.bfloat16)).astype(jnp.float32)
        grad_gatein = lax.optimization_barrier((grad_hidden * upval * sig * (1.0 + gate * (1.0 - sig))).astype(jnp.bfloat16)).astype(jnp.float32)
        grad_down = jnp.dot(hidden.T, slot_go, preferred_element_type=jnp.float32)
        grad_gate = jnp.dot(grad_gatein.T, slot_in, preferred_element_type=jnp.float32)
        grad_up = jnp.dot(grad_upin.T, slot_in, preferred_element_type=jnp.float32)
        total = jnp.zeros(slot_in.shape, jnp.float32)
        for which in range(N_TP):
            lo = which * block
            hi = lo + block
            part = jnp.dot(grad_gatein[:, lo:hi], wg32[lo:hi], preferred_element_type=jnp.float32)
            part = part + jnp.dot(grad_upin[:, lo:hi], wu32[lo:hi], preferred_element_type=jnp.float32)
            total = total + lax.optimization_barrier(part.astype(jnp.bfloat16)).astype(jnp.float32)
        return total.astype(jnp.bfloat16), grad_gate, grad_up, grad_down

    slot_grads, grad_gate, grad_up, grad_down = lax.map(expert, (owner, gate_weight, up_weight, down_weight))
    per_pick = slot_grads[flat_ids, flat_place].astype(jnp.float32)
    grad_tokens = jnp.sum(per_pick.reshape(TOKENS, TOP, D), axis=1).astype(jnp.bfloat16)
    return grad_tokens, grad_gate, grad_up, grad_down
```

```python
import functools

import jax
import jax.numpy as jnp
from jax import lax
from jax.experimental import pallas as pl
from jax.experimental.pallas import tpu as pltpu
from jax.sharding import PartitionSpec as P

F32 = jnp.float32
BF16 = jnp.bfloat16
ROWS_LAST = (((1,), (1,)), ((), ()))


def flip(c, d, n):
    total, b = 0, 1
    while b < n:
        bit = (c // b) % 2
        total = total + ((1 - bit) if d & b else bit) * b
        b *= 2
    return total


def positions(n_tp):
    c = lax.axis_index("cp")
    t = lax.axis_index("tp")
    n_y = n_tp // 2
    k = t % 2
    y = t // 2
    return c, t, n_y, k, y


def greet(n_cp, n_tp):
    c, t, n_y, k, y = positions(n_tp)
    barrier = pltpu.get_barrier_semaphore()
    peers = [(flip(c, d, n_cp), t) for d in range(1, n_cp)]
    peers += [(c, ((y + dy) % n_y) * 2 + k) for dy in range(1, n_y)]
    peers += [(c, y * 2 + 1 - k)]
    for peer in peers:
        pl.semaphore_signal(barrier, inc=1, device_id=peer, device_id_type=pl.DeviceIdType.MESH)
    pl.semaphore_wait(barrier, len(peers))


def remote(src, dst, send, recv, peer):
    return pltpu.make_async_remote_copy(
        src_ref=src, dst_ref=dst, send_sem=send, recv_sem=recv,
        device_id=peer, device_id_type=pl.DeviceIdType.MESH,
    )


def slot_of(ids, slots):
    n = ids.shape[1]
    mine = ids.astype(F32)
    here = jnp.broadcast_to(mine, (n, n))
    there = here.T
    earlier = lax.broadcasted_iota(jnp.int32, (n, n), 0) < lax.broadcasted_iota(jnp.int32, (n, n), 1)
    rank = jnp.sum(jnp.where((here == there) & earlier, 1.0, 0.0), axis=0, keepdims=True)
    return mine * slots + rank


def column(row):
    n = row.shape[1]
    return jnp.broadcast_to(row, (n, n)).T[:, :1]


def queue(n_cp):
    far = list(range(n_cp // 2, n_cp))
    near = list(range(1, n_cp // 2))
    out = [0]
    for i, f in enumerate(far):
        out += near[i:i + 1] + [f]
    return out


def plan(n_cp):
    q = queue(n_cp)
    near = list(range(1, n_cp // 2))
    far = list(range(n_cp // 2, n_cp))
    last, before = q[-1], q[-2]
    steps = [("A", 0)]
    for i in range(1, n_cp - 1):
        steps += [("A", q[i]), ("B", q[i - 1])]
        if i > 1 and q[i - 2] in far:
            steps += [("E", q[i - 2])]
        steps += [("C", q[i - 1]), ("D", q[i - 1])]
    held = [d for d in far if d not in (last, before)]
    steps += [("B", before), ("A", last)] + [("F", d) for d in held]
    steps += [("C", before), ("D", before), ("E", before), ("E", near[0])]
    steps += [("B", last), ("C", last), ("D", last), ("F", before), ("E", last)]
    steps += [("E", d) for d in near[1:]] + [("E", 0), ("T", 0)]
    steps += [("F", near[0]), ("F", last)] + [("F", d) for d in near[1:]] + [("F", 0)]
    return steps


def fused_kernel(
    n_cp, n_tp, slots,
    ids, wts, tok_h, go_h, wg_h, wu_h, wd_h,
    got, acts_o, out,
    tokv, wg, wu, wd, xg, buf, p, a, sb, yb, tb, acts, acts_t,
    t_sem, w_sem, l_sem, loc, o_sem, cp_s, cp_r, y_s, y_r, s_s, s_r, f_s, f_r,
    rs_s, rs_r, ry_s, ry_r, rc_s, rc_r,
):
    c, t, n_y, k, y = positions(n_tp)
    sib = y * 2 + 1 - k
    rows = n_tp * slots
    width = xg.shape[-1]
    step = 512

    tok_loads = [
        pltpu.make_async_copy(h, tokv.at[i], t_sem.at[i]) for i, h in enumerate((tok_h, go_h))
    ]
    loads = [
        pltpu.make_async_copy(h, v, w_sem.at[i])
        for i, (h, v) in enumerate(((wg_h, wg), (wu_h, wu), (wd_h, wd)))
    ]
    for copy in tok_loads:
        copy.start()
    greet(n_cp, n_tp)

    place = slot_of(ids[...], slots)
    at_rows = lax.broadcasted_iota(jnp.int32, (n_cp * slots, place.shape[1]), 0).astype(F32)
    placer = jnp.where(at_rows == place, 1.0, 0.0).astype(BF16)
    weight = column(wts[...])
    for copy in tok_loads:
        copy.wait()

    def fill(i, carry):
        cols = pl.ds(pl.multiple_of(i * step, step), step)
        g = (weight * tokv[1, :, cols].astype(F32)).astype(BF16)
        for which, rhs in ((0, tokv[0, :, cols]), (1, g)):
            v = jnp.dot(placer, rhs, preferred_element_type=F32)
            for e in range(n_cp):
                xg[which, e, :, cols] = v[e * slots:(e + 1) * slots].astype(BF16)
        return carry

    lax.fori_loop(0, width // step, fill, 0)

    def cell(s, tt):
        return got.at[:, pl.ds(pl.multiple_of((s * n_tp + tt) * slots, 8), slots)]

    def cp_copy(d):
        peer = flip(c, d, n_cp)
        return remote(xg.at[:, peer], cell(c, t), cp_s.at[d], cp_r.at[d], (peer, t))

    def have(d):
        return xg.at[:, c] if d == 0 else cell(flip(c, d, n_cp), t)

    def y_copy(d, dy):
        to = ((y + dy) % n_y) * 2 + k
        return remote(have(d), cell(flip(c, d, n_cp), t), y_s.at[d, dy], y_r.at[d, dy], (c, to))

    def s_copy(d):
        return remote(have(d), cell(flip(c, d, n_cp), t), s_s.at[d], s_r.at[d], (c, sib))

    def f_copy(d, dy):
        part = cell(flip(c, d, n_cp), ((y + n_y - dy) % n_y) * 2 + k)
        return remote(part, part, f_s.at[d, dy], f_r.at[d, dy], (c, sib))

    def rs_copy(d, yy):
        return remote(
            p.at[d * n_tp + yy * 2 + 1 - k], a.at[d * n_y + yy],
            rs_s.at[d, yy], rs_r.at[d, yy], (c, sib),
        )

    def ry_copy(d, dy):
        to = ((y + dy) % n_y) * 2 + k
        return remote(sb.at[d, dy - 1], yb.at[d, dy - 1], ry_s.at[d, dy], ry_r.at[d, dy], (c, to))

    def rc_copy(d):
        peer = flip(c, d, n_cp)
        return remote(tb.at[d], out.at[c], rc_s.at[d], rc_r.at[d], (peer, t))

    def pair(d, yy):
        return p[d * n_tp + yy * 2 + k].astype(F32) + a[d * n_y + yy].astype(F32)

    def chunk_rows(d):
        return pl.ds(pl.multiple_of(flip(c, d, n_cp) * rows, 16), rows)

    def compute(d, slot):
        at = chunk_rows(d)
        x = buf[slot, 0]
        gate = lax.dot_general(x, wg[...], ROWS_LAST, preferred_element_type=F32)
        upval = lax.dot_general(x, wu[...], ROWS_LAST, preferred_element_type=F32)
        gh = lax.dot_general(buf[slot, 1], wd[...], ROWS_LAST, preferred_element_type=F32)
        sig = jax.nn.sigmoid(gate)
        act = gate * sig
        acts[0, at] = (act * upval).astype(BF16)
        acts[2, at] = (gh * act).astype(BF16)
        acts[1, at] = (gh * upval * sig * (1.0 + gate * (1.0 - sig))).astype(BF16)

        def tile(i, carry):
            cols = pl.ds(pl.multiple_of(i * step, step), step)
            v = jnp.dot(acts[1, at], wg[:, cols], preferred_element_type=F32)
            v = v + jnp.dot(acts[2, at], wu[:, cols], preferred_element_type=F32)
            for tt in range(n_tp):
                p[d * n_tp + tt, :, cols] = v[tt * slots:(tt + 1) * slots].astype(BF16)
            return carry

        lax.fori_loop(0, width // step, tile, 0)

    own = pltpu.make_async_copy(xg.at[:, c], cell(c, t), loc.at[0])
    home = pltpu.make_async_copy(tb.at[0], out.at[c], loc.at[1])
    acts_out = [pltpu.make_async_copy(acts_t.at[i], acts_o.at[i], o_sem.at[i]) for i in range(3)]
    order = queue(n_cp)
    computed = [d for stage, d in plan(n_cp) if stage == "D"]

    def chunk_load(d, slot):
        return pltpu.make_async_copy(got.at[:, chunk_rows(d)], buf.at[slot], l_sem.at[slot])

    for stage, d in plan(n_cp):
        slot = computed.index(d) % 2
        if stage == "A":
            if d:
                cp_copy(d).wait_recv()
            for dy in range(1, n_y):
                y_copy(d, dy).start()
            s_copy(d).start()
            if d == 0:
                for e in order[1:]:
                    cp_copy(e).start()
                own.start()
                for copy in loads:
                    copy.start()
        if stage == "B":
            for dy in range(1, n_y):
                y_copy(d, dy).wait_recv()
                f_copy(d, dy).start()
        if stage == "C":
            s_copy(d).wait_recv()
            for dy in range(1, n_y):
                f_copy(d, dy).wait_recv()
            if d == 0:
                own.wait()
            chunk_load(d, slot).start()
        if stage == "D":
            if d == computed[0]:
                for copy in loads:
                    copy.wait()
            chunk_load(d, slot).wait()
            compute(d, slot)
            for yy in range(n_y):
                rs_copy(d, yy).start()
        if stage == "E":
            for yy in range(n_y):
                rs_copy(d, yy).wait_recv()
            for dy in range(1, n_y):
                sb[d, dy - 1] = pair(d, (y + dy) % n_y).astype(BF16)
                ry_copy(d, dy).start()
        if stage == "F":
            total = pair(d, y)
            for dy in range(1, n_y):
                ry_copy(d, dy).wait_recv()
                total = total + yb[d, dy - 1].astype(F32)
            tb[d] = total.astype(BF16)
            if d:
                rc_copy(d).start()
            else:
                home.start()
        if stage == "T":
            for i in range(3):
                acts_t[i] = acts[i].T
                acts_out[i].start()
    home.wait()
    for copy in acts_out:
        copy.wait()
    for d in range(n_cp):
        if d:
            cp_copy(d).wait_send()
            rc_copy(d).wait()
        s_copy(d).wait_send()
        for dy in range(1, n_y):
            y_copy(d, dy).wait_send()
            f_copy(d, dy).wait_send()
            ry_copy(d, dy).wait_send()
        for yy in range(n_y):
            rs_copy(d, yy).wait_send()


def fused(ids, wts, tokens, grad_out, w_gate, w_up, w_down, n_cp, n_tp, slots):
    count, width = tokens.shape
    hid = w_gate.shape[0]
    n_y = n_tp // 2
    rows = n_tp * slots
    total = n_cp * rows
    dma = pltpu.SemaphoreType.DMA
    anyspace = pl.BlockSpec(memory_space=pl.ANY)
    vmem = pl.BlockSpec(memory_space=pltpu.VMEM)
    one = dma((n_cp,))
    two = dma((n_cp, n_y))
    return pl.pallas_call(
        functools.partial(fused_kernel, n_cp, n_tp, slots),
        out_shape=(
            jax.ShapeDtypeStruct((2, total, width), BF16),
            jax.ShapeDtypeStruct((3, hid, total), BF16),
            jax.ShapeDtypeStruct((n_cp, slots, width), BF16),
        ),
        in_specs=[vmem, vmem] + [anyspace] * 5,
        out_specs=(anyspace,) * 3,
        scratch_shapes=[
            pltpu.VMEM((2, count, width), BF16),
            pltpu.VMEM((hid, width), BF16),
            pltpu.VMEM((hid, width), BF16),
            pltpu.VMEM((hid, width), BF16),
            pltpu.VMEM((2, n_cp, slots, width), BF16),
            pltpu.VMEM((2, 2, rows, width), BF16),
            pltpu.VMEM((n_cp * n_tp, slots, width), BF16),
            pltpu.VMEM((n_cp * n_y, slots, width), BF16),
            pltpu.VMEM((n_cp, n_y - 1, slots, width), BF16),
            pltpu.VMEM((n_cp, n_y - 1, slots, width), BF16),
            pltpu.VMEM((n_cp, slots, width), BF16),
            pltpu.VMEM((3, total, hid), BF16),
            pltpu.VMEM((3, hid, total), BF16),
            dma((2,)), dma((3,)), dma((2,)), dma((2,)), dma((3,)),
            one, one, two, two, one, one, two, two, two, two, two, two, one, one,
        ],
        compiler_params=pltpu.CompilerParams(
            collective_id=0, has_side_effects=True, vmem_limit_bytes=60 << 20
        ),
        cost_estimate=pl.CostEstimate(
            flops=10 * total * hid * width, bytes_accessed=8 * total * width,
            transcendentals=total * hid,
        ),
        name="fused",
    )(ids, wts, tokens, grad_out, w_gate, w_up, w_down)


def last_kernel(slots, ids, xg, acts_t, sg, d_gate, d_up, d_down, d_tok, picker):
    @pl.when(pl.program_id(0) == 0)
    def _():
        place = column(slot_of(ids[...], slots))
        at = lax.broadcasted_iota(jnp.int32, picker.shape, 1).astype(F32)
        picker[...] = jnp.where(at == place, 1.0, 0.0).astype(BF16)

    x = xg[0]
    d_gate[...] = jnp.dot(acts_t[1], x, preferred_element_type=F32)
    d_up[...] = jnp.dot(acts_t[2], x, preferred_element_type=F32)
    d_down[...] = jnp.dot(acts_t[0], xg[1], preferred_element_type=F32)
    d_tok[...] = jnp.dot(picker[...], sg[...], preferred_element_type=F32).astype(BF16)


def last(ids, got, acts_t, slot_grad, slots):
    _, total, width = got.shape
    hid = acts_t.shape[1]
    count = ids.shape[1]
    cells = slot_grad.shape[0]
    step = 512
    grad = pl.BlockSpec((hid, step), lambda i: (0, i))
    shape = jax.ShapeDtypeStruct((hid, width), F32)
    return pl.pallas_call(
        functools.partial(last_kernel, slots),
        grid=(width // step,),
        out_shape=(shape,) * 3 + (jax.ShapeDtypeStruct((count, width), BF16),),
        in_specs=[
            pl.BlockSpec((1, count), lambda i: (0, 0)),
            pl.BlockSpec((2, total, step), lambda i: (0, 0, i)),
            pl.BlockSpec((3, hid, total), lambda i: (0, 0, 0)),
            pl.BlockSpec((cells, step), lambda i: (0, i)),
        ],
        out_specs=(grad,) * 3 + (pl.BlockSpec((count, step), lambda i: (0, i)),),
        scratch_shapes=[pltpu.VMEM((count, cells), BF16)],
        compiler_params=pltpu.CompilerParams(vmem_limit_bytes=48 << 20),
        cost_estimate=pl.CostEstimate(
            flops=6 * total * hid * width + 2 * count * cells * width,
            bytes_accessed=4 * total * width + 12 * hid * width + 2 * (cells + count) * width,
            transcendentals=0,
        ),
        name="last",
    )(ids, got, acts_t, slot_grad)


def body(tokens, grad_out, expert_ids, router_weights, gate_weight, up_weight, down_weight):
    n_cp = lax.axis_size("cp")
    n_tp = lax.axis_size("tp")
    count, width = tokens.shape
    slots = -(-max(2, 3 * count // (2 * n_cp)) // 8) * 8
    ids = expert_ids.reshape(1, count)
    wts = router_weights.reshape(1, count)
    got, acts_t, slot_grad = fused(
        ids, wts, tokens, grad_out, gate_weight[0], up_weight[0], down_weight[0], n_cp, n_tp, slots
    )
    grad_gate, grad_up, grad_down, grad_tokens = last(
        ids, got, acts_t, slot_grad.reshape(n_cp * slots, width), slots
    )
    return (grad_tokens, grad_gate[None], grad_up[None], grad_down[None])


def solution(mesh):
    tok = P(("cp", "tp"), None)
    wgt = P("cp", "tp", None)
    return jax.shard_map(
        body,
        mesh=mesh,
        in_specs=(tok, tok, tok, tok, wgt, wgt, wgt),
        out_specs=(tok, wgt, wgt, wgt),
        check_vma=False,
    )
```

```python
import functools

import jax
import jax.numpy as jnp
from jax import lax
from jax.experimental import pallas as pl
from jax.experimental.pallas import tpu as pltpu
from jax.sharding import PartitionSpec as P

F32 = jnp.float32
BF16 = jnp.bfloat16
ROWS_LAST = (((1,), (1,)), ((), ()))


def flip(c, d, n):
    total, b = 0, 1
    while b < n:
        bit = (c // b) % 2
        total = total + ((1 - bit) if d & b else bit) * b
        b *= 2
    return total


def positions(n_tp):
    c = lax.axis_index("cp")
    t = lax.axis_index("tp")
    n_y = n_tp // 2
    k = t % 2
    y = t // 2
    return c, t, n_y, k, y


def greet(n_cp, n_tp):
    c, t, n_y, k, y = positions(n_tp)
    barrier = pltpu.get_barrier_semaphore()
    peers = [(flip(c, d, n_cp), t) for d in range(1, n_cp)]
    peers += [(c, ((y + dy) % n_y) * 2 + k) for dy in range(1, n_y)]
    peers += [(c, y * 2 + 1 - k)]
    for peer in peers:
        pl.semaphore_signal(barrier, inc=1, device_id=peer, device_id_type=pl.DeviceIdType.MESH)
    pl.semaphore_wait(barrier, len(peers))


def remote(src, dst, send, recv, peer):
    return pltpu.make_async_remote_copy(
        src_ref=src, dst_ref=dst, send_sem=send, recv_sem=recv,
        device_id=peer, device_id_type=pl.DeviceIdType.MESH,
    )


def tiles_of(total, width):
    return width // (512 if total <= 1024 else 128)


def slot_of(ids, slots):
    n = ids.shape[1]
    mine = ids.astype(F32)
    here = jnp.broadcast_to(mine, (n, n))
    there = here.T
    earlier = lax.broadcasted_iota(jnp.int32, (n, n), 0) < lax.broadcasted_iota(jnp.int32, (n, n), 1)
    rank = jnp.sum(jnp.where((here == there) & earlier, 1.0, 0.0), axis=0, keepdims=True)
    return mine * slots + rank


def column(row):
    n = row.shape[1]
    return jnp.broadcast_to(row, (n, n)).T[:, :1]


def queue(n_cp):
    far = list(range(n_cp // 2, n_cp))
    near = list(range(1, n_cp // 2))
    out = [0]
    for i, f in enumerate(far):
        out += near[i:i + 1] + [f]
    return out


def plan(n_cp, tiles):
    q = queue(n_cp)
    near = list(range(1, n_cp // 2))
    far = list(range(n_cp // 2, n_cp))
    last, before = q[-1], q[-2]
    steps = [("A", 0)]
    for i in range(1, n_cp - 1):
        steps += [("A", q[i]), ("B", q[i - 1])]
        if i > 1 and q[i - 2] in far:
            steps += [("E", q[i - 2])]
        steps += [("C", q[i - 1]), ("D", q[i - 1])]
    held = [d for d in far if d not in (last, before)]
    steps += [("B", before), ("A", last)] + [("F", d) for d in held]
    steps += [("C", before), ("D", before), ("E", before), ("E", near[0])]
    steps += [("B", last), ("C", last), ("D", last), ("F", before), ("E", last)]
    steps += [("E", d) for d in near[1:]] + [("E", 0), ("T", 0), ("F", near[0]), ("W", 0), ("F", last)]
    rest = near[1:] + [0]
    done = 1
    for i, d in enumerate(rest):
        upto = 1 + (i + 1) * (tiles - 1) // len(rest)
        steps += [("W", j) for j in range(done, upto)] + [("F", d)]
        done = upto
    return steps


def fused_kernel(
    n_cp, n_tp, slots,
    ids, wts, tok_h, go_h, wg_h, wu_h, wd_h,
    got, grads, out,
    wg, wu, wd, xg, buf, p, a, yb, acts, acts_t, xb,
    t_sem, w_sem, l_sem, loc, x_sem, cp_s, cp_r, y_s, y_r, s_s, s_r, f_s, f_r,
    rs_s, rs_r, ry_s, ry_r, rc_s, rc_r,
):
    c, t, n_y, k, y = positions(n_tp)
    sib = y * 2 + 1 - k
    rows = n_tp * slots
    width = xg.shape[-1]
    step = 512
    count = tok_h.shape[0]
    tiles = tiles_of(n_cp * rows, width)
    wide = width // tiles
    tok_loads = [
        pltpu.make_async_copy(h, buf.at[0, i, pl.ds(0, count)], t_sem.at[i])
        for i, h in enumerate((tok_h, go_h))
    ]
    loads = [
        pltpu.make_async_copy(h, v, w_sem.at[i])
        for i, (h, v) in enumerate(((wg_h, wg), (wu_h, wu), (wd_h, wd)))
    ]
    for copy in tok_loads:
        copy.start()
    greet(n_cp, n_tp)

    place = slot_of(ids[...], slots)
    at_rows = lax.broadcasted_iota(jnp.int32, (n_cp * slots, place.shape[1]), 0).astype(F32)
    placer = jnp.where(at_rows == place, 1.0, 0.0).astype(BF16)
    weight = column(wts[...])
    for copy in tok_loads:
        copy.wait()

    def fill(i, carry):
        cols = pl.ds(pl.multiple_of(i * step, step), step)
        g = (weight * buf[0, 1, :count, cols].astype(F32)).astype(BF16)
        for which, rhs in ((0, buf[0, 0, :count, cols]), (1, g)):
            v = jnp.dot(placer, rhs, preferred_element_type=F32)
            for e in range(n_cp):
                xg[which, e, :, cols] = v[e * slots:(e + 1) * slots].astype(BF16)
        return carry

    lax.fori_loop(0, width // step, fill, 0)

    def cell(s, tt):
        return got.at[:, pl.ds(pl.multiple_of((s * n_tp + tt) * slots, 8), slots)]

    def cp_copy(d):
        peer = flip(c, d, n_cp)
        return remote(xg.at[:, peer], cell(c, t), cp_s.at[d], cp_r.at[d], (peer, t))

    def have(d):
        return xg.at[:, c] if d == 0 else cell(flip(c, d, n_cp), t)

    def y_copy(d, dy):
        to = ((y + dy) % n_y) * 2 + k
        return remote(have(d), cell(flip(c, d, n_cp), t), y_s.at[d, dy], y_r.at[d, dy], (c, to))

    def s_copy(d):
        return remote(have(d), cell(flip(c, d, n_cp), t), s_s.at[d], s_r.at[d], (c, sib))

    def f_copy(d, dy):
        part = cell(flip(c, d, n_cp), ((y + n_y - dy) % n_y) * 2 + k)
        return remote(part, part, f_s.at[d, dy], f_r.at[d, dy], (c, sib))

    def rs_copy(d, yy):
        return remote(
            p.at[d * n_tp + yy * 2 + 1 - k], a.at[d * n_y + yy],
            rs_s.at[d, yy], rs_r.at[d, yy], (c, sib),
        )

    def ry_copy(d, dy):
        to = ((y + dy) % n_y) * 2 + k
        src = a.at[d * n_y + (y + dy) % n_y]
        return remote(src, yb.at[d, dy - 1], ry_s.at[d, dy], ry_r.at[d, dy], (c, to))

    def rc_copy(d):
        peer = flip(c, d, n_cp)
        return remote(a.at[d * n_y + y], out.at[c], rc_s.at[d], rc_r.at[d], (peer, t))

    def pair(d, yy):
        return p[d * n_tp + yy * 2 + k].astype(F32) + a[d * n_y + yy].astype(F32)

    def chunk_rows(d):
        return pl.ds(pl.multiple_of(flip(c, d, n_cp) * rows, 16), rows)

    def compute(d, slot):
        at = chunk_rows(d)
        x = buf[slot, 0, :rows]
        gate = lax.dot_general(x, wg[...], ROWS_LAST, preferred_element_type=F32)
        upval = lax.dot_general(x, wu[...], ROWS_LAST, preferred_element_type=F32)
        gh = lax.dot_general(buf[slot, 1, :rows], wd[...], ROWS_LAST, preferred_element_type=F32)
        sig = jax.nn.sigmoid(gate)
        act = gate * sig
        acts[0, at] = (act * upval).astype(BF16)
        acts[2, at] = (gh * act).astype(BF16)
        acts[1, at] = (gh * upval * sig * (1.0 + gate * (1.0 - sig))).astype(BF16)

        def tile(i, carry):
            cols = pl.ds(pl.multiple_of(i * step, step), step)
            v = jnp.dot(acts[1, at], wg[:, cols], preferred_element_type=F32)
            v = v + jnp.dot(acts[2, at], wu[:, cols], preferred_element_type=F32)
            for tt in range(n_tp):
                p[d * n_tp + tt, :, cols] = v[tt * slots:(tt + 1) * slots].astype(BF16)
            return carry

        lax.fori_loop(0, width // step, tile, 0)

    own = pltpu.make_async_copy(xg.at[:, c], cell(c, t), loc.at[0])
    home = pltpu.make_async_copy(a.at[y], out.at[c], loc.at[1])
    order = queue(n_cp)
    after = {}
    for line in (range(1, n_cp // 2), range(n_cp // 2, n_cp)):
        for j, d in enumerate(line):
            if j:
                after[line[j - 1]] = d
    steps = plan(n_cp, tiles)
    computed = [d for stage, d in steps if stage == "D"]

    def chunk_load(d, slot):
        return pltpu.make_async_copy(got.at[:, chunk_rows(d)], buf.at[slot, :, pl.ds(0, rows)], l_sem.at[slot])

    def tile_load(j):
        src = got.at[:, :, pl.ds(j * wide, wide)]
        return pltpu.make_async_copy(src, xb.at[j % 2], x_sem.at[j % 2])

    for stage, d in steps:
        slot = computed.index(d) % 2 if stage != "W" else 0
        if stage == "A":
            if d:
                cp_copy(d).wait_recv()
            for dy in range(1, n_y):
                y_copy(d, dy).start()
            s_copy(d).start()
            if d in after:
                cp_copy(after[d]).start()
            if d == 0:
                for e in order[1:]:
                    if e not in after.values():
                        cp_copy(e).start()
                own.start()
                for copy in loads:
                    copy.start()
        if stage == "B":
            for dy in range(1, n_y):
                y_copy(d, dy).wait_recv()
                f_copy(d, dy).start()
        if stage == "C":
            s_copy(d).wait_recv()
            for dy in range(1, n_y):
                f_copy(d, dy).wait_recv()
            if d == 0:
                own.wait()
            chunk_load(d, slot).start()
        if stage == "D":
            if d == computed[0]:
                for copy in loads:
                    copy.wait()
            chunk_load(d, slot).wait()
            compute(d, slot)
            for yy in range(n_y):
                rs_copy(d, yy).start()
        if stage == "E":
            for yy in range(n_y):
                rs_copy(d, yy).wait_recv()
            for dy in range(1, n_y):
                yy = (y + dy) % n_y
                a[d * n_y + yy] = pair(d, yy).astype(BF16)
                ry_copy(d, dy).start()
        if stage == "F":
            total = pair(d, y)
            for dy in range(1, n_y):
                ry_copy(d, dy).wait_recv()
                total = total + yb[d, dy - 1].astype(F32)
            a[d * n_y + y] = total.astype(BF16)
            if d:
                rc_copy(d).start()
            else:
                home.start()
        if stage == "T":
            tile_load(0).start()
            for i in range(3):
                acts_t[i] = acts[i].T
        if stage == "W":
            if d + 1 < tiles:
                tile_load(d + 1).start()
            tile_load(d).wait()
            cols = pl.ds(d * wide, wide)
            for i, which in ((0, 1), (1, 0), (2, 0)):
                grads[i, :, cols] = jnp.dot(acts_t[i], xb[d % 2, which], preferred_element_type=F32)
    home.wait()
    for d in range(n_cp):
        if d:
            cp_copy(d).wait_send()
            rc_copy(d).wait()
        s_copy(d).wait_send()
        for dy in range(1, n_y):
            y_copy(d, dy).wait_send()
            f_copy(d, dy).wait_send()
            ry_copy(d, dy).wait_send()
        for yy in range(n_y):
            rs_copy(d, yy).wait_send()


def fused(ids, wts, tokens, grad_out, w_gate, w_up, w_down, n_cp, n_tp, slots):
    count, width = tokens.shape
    hid = w_gate.shape[0]
    n_y = n_tp // 2
    rows = n_tp * slots
    total = n_cp * rows
    dma = pltpu.SemaphoreType.DMA
    anyspace = pl.BlockSpec(memory_space=pl.ANY)
    vmem = pl.BlockSpec(memory_space=pltpu.VMEM)
    one = dma((n_cp,))
    two = dma((n_cp, n_y))
    return pl.pallas_call(
        functools.partial(fused_kernel, n_cp, n_tp, slots),
        out_shape=(
            jax.ShapeDtypeStruct((2, total, width), BF16),
            pltpu.VMEM((3, hid, width), F32),
            pltpu.VMEM((n_cp, slots, width), BF16),
        ),
        in_specs=[vmem, vmem] + [anyspace] * 5,
        out_specs=(anyspace, vmem, vmem),
        scratch_shapes=[
            pltpu.VMEM((hid, width), BF16),
            pltpu.VMEM((hid, width), BF16),
            pltpu.VMEM((hid, width), BF16),
            pltpu.VMEM((2, n_cp, slots, width), BF16),
            pltpu.VMEM((2, 2, max(rows, count), width), BF16),
            pltpu.VMEM((n_cp * n_tp, slots, width), BF16),
            pltpu.VMEM((n_cp * n_y, slots, width), BF16),
            pltpu.VMEM((n_cp, n_y - 1, slots, width), BF16),
            pltpu.VMEM((3, total, hid), BF16),
            pltpu.VMEM((3, hid, total), BF16),
            pltpu.VMEM((2, 2, total, width // tiles_of(total, width)), BF16),
            dma((2,)), dma((3,)), dma((2,)), dma((2,)), dma((2,)),
            one, one, two, two, one, one, two, two, two, two, two, two, one, one,
        ],
        compiler_params=pltpu.CompilerParams(
            collective_id=0, has_side_effects=True,
            vmem_limit_bytes=(62 << 20) - 12 * hid * width - 2 * n_cp * slots * width,
        ),
        cost_estimate=pl.CostEstimate(
            flops=16 * total * hid * width, bytes_accessed=12 * total * width,
            transcendentals=total * hid,
        ),
        name="fused",
    )(ids, wts, tokens, grad_out, w_gate, w_up, w_down)


def last_kernel(slots, ids, grads, sg, d_gate, d_up, d_down, d_tok, tok, t_sem, o_sem):
    outs = [
        pltpu.make_async_copy(grads.at[i], o, o_sem.at[i]) for i, o in enumerate((d_down, d_gate, d_up))
    ]
    for copy in outs:
        copy.start()
    place = column(slot_of(ids[...], slots))
    at = lax.broadcasted_iota(jnp.int32, (tok.shape[0], sg.shape[0]), 1).astype(F32)
    picker = jnp.where(at == place, 1.0, 0.0).astype(BF16)
    step = 512

    def tile(i, carry):
        cols = pl.ds(pl.multiple_of(i * step, step), step)
        tok[:, cols] = jnp.dot(picker, sg[:, cols], preferred_element_type=F32).astype(BF16)
        return carry

    lax.fori_loop(0, tok.shape[1] // step, tile, 0)
    done = pltpu.make_async_copy(tok, d_tok, t_sem)
    done.start()
    done.wait()
    for copy in outs:
        copy.wait()


def last(ids, grads, slot_grad, slots):
    _, hid, width = grads.shape
    count = ids.shape[1]
    cells = slot_grad.shape[0]
    anyspace = pl.BlockSpec(memory_space=pl.ANY)
    vmem = pl.BlockSpec(memory_space=pltpu.VMEM)
    shape = jax.ShapeDtypeStruct((hid, width), F32)
    return pl.pallas_call(
        functools.partial(last_kernel, slots),
        out_shape=(shape,) * 3 + (jax.ShapeDtypeStruct((count, width), BF16),),
        in_specs=[vmem, vmem, vmem],
        out_specs=(anyspace,) * 4,
        scratch_shapes=[
            pltpu.VMEM((count, width), BF16),
            pltpu.SemaphoreType.DMA, pltpu.SemaphoreType.DMA((3,)),
        ],
        compiler_params=pltpu.CompilerParams(vmem_limit_bytes=16 << 20),
        cost_estimate=pl.CostEstimate(
            flops=2 * count * cells * width,
            bytes_accessed=12 * hid * width + 2 * (cells + count) * width,
            transcendentals=0,
        ),
        name="last",
    )(
        ids,
        pltpu.with_memory_space_constraint(grads, pltpu.VMEM),
        pltpu.with_memory_space_constraint(slot_grad, pltpu.VMEM),
    )


def body(tokens, grad_out, expert_ids, router_weights, gate_weight, up_weight, down_weight):
    n_cp = lax.axis_size("cp")
    n_tp = lax.axis_size("tp")
    count, width = tokens.shape
    slots = -(-max(2, 3 * count // (2 * n_cp)) // 8) * 8
    ids = expert_ids.reshape(1, count)
    wts = router_weights.reshape(1, count)
    _, grads, slot_grad = fused(
        ids, wts, tokens, grad_out, gate_weight[0], up_weight[0], down_weight[0], n_cp, n_tp, slots
    )
    grad_gate, grad_up, grad_down, grad_tokens = last(
        ids, grads, slot_grad.reshape(n_cp * slots, width), slots
    )
    return (grad_tokens, grad_gate[None], grad_up[None], grad_down[None])


def solution(mesh):
    tok = P(("cp", "tp"), None)
    wgt = P("cp", "tp", None)
    return jax.shard_map(
        body,
        mesh=mesh,
        in_specs=(tok, tok, tok, tok, wgt, wgt, wgt),
        out_specs=(tok, wgt, wgt, wgt),
        check_vma=False,
    )
```
